512 devices in a mesh: row: 64 (over x, y, core), col: 8 (over z).
Axes of the slice: x: 4, y: 8, z: 8, core: 2. Of those that a mesh axis runs over, the one named last changes fastest.
Arguments:
- panel: float32 [49152, 512], P(('row', 'col')), may hold values from -600 to 600
- trailing: float32 [49152, 4096], P('row', 'col'), may hold values from -6 to 6
Outputs:
- r_factor: float32 [512, 512], replicated
- residual: float32 [49152, 4096], P('row', 'col')
The draws below stay inside these ranges and needn't reach their ends.
All inputs are finite; a program needn't handle non-finite values.
Results may differ from the reference program's by a relative error of at most 0.0003.
Values sent between devices are 32-bit elements; how exact they have to be, the bound alone decides.
No kernel may reach another device: no remote copies, remote signals or barrier semaphores. Data moves between devices by JAX's collectives and lax.ppermute only.
A program may use at most 64 MiB of HBM per device.

```python
import math
import jax
import jax.numpy as jnp
from jax import lax

B = 512
NROWS = 49152
NTRAIL = 4096


def draw_panel(key, part):
    keys = jax.random.split(key, 4)
    base = jax.random.normal(keys[0], (NROWS, B), jnp.float32)
    spread = 10.0
    mixing = jax.random.normal(keys[1], (B, B), jnp.float32) * (0.3 / math.sqrt(B))
    mixed = base + jnp.dot(base, mixing, precision=lax.Precision.HIGHEST)
    position = jnp.arange(NROWS, dtype=jnp.float32) / NROWS
    row_scale = jnp.exp(jax.random.uniform(keys[2], (NROWS,), jnp.float32, 0.0, math.log(spread))) * (1.0 + 2.0 * position)
    col_scale = jnp.exp(jax.random.uniform(keys[3], (B,), jnp.float32, 0.0, math.log(10.0)))
    return mixed * row_scale[:, None] * col_scale[None, :] * 0.1


def levels(stream_key, extent, cuts, least, largest):
    def one(dim, shards_of):
        steps = jax.random.uniform(jax.random.fold_in(jax.random.fold_in(stream_key, 6), dim), (shards_of,), jnp.float32, least / len(cuts), largest / len(cuts))
        return jnp.repeat(jnp.exp(steps), extent[dim] // shards_of).reshape((-1,) + (1,) * (len(extent) - dim - 1))

    loudness = one(*cuts[0])
    for cut in cuts[1:]:
        loudness = loudness * one(*cut)
    return loudness


def centred(own_key, dims, scale, most, shards=(), kind=jnp.bfloat16):
    gain = levels(own_key, dims, shards, -0.22, 0.18) if shards else 1.0
    values = jax.random.normal(own_key, dims, jnp.float32) * scale * gain
    return jnp.minimum(jnp.maximum(values, -most), most).astype(kind)


def setup_inputs(seed: int = 0) -> dict:
    arg_keys = jax.random.split(jax.random.key(seed), 3)
    panel = draw_panel(jax.random.fold_in(arg_keys[2], 71), 0)
    trailing = centred(arg_keys[1], (NROWS, NTRAIL), 1.0, 6.0, ((0, 64), (1, 8)), jnp.float32)
    return dict(panel=panel, trailing=trailing)


def reference(panel, trailing):
    basis, upper = jnp.linalg.qr(panel)
    signs = jnp.sign(jnp.diagonal(upper))
    upper = upper * signs[:, None]
    basis = basis * signs[None, :]
    coupling = jnp.dot(basis.T.astype(jnp.float32), trailing.astype(jnp.float32), precision=lax.Precision.HIGHEST, preferred_element_type=jnp.float32)
    residual = trailing - jnp.dot(basis.astype(jnp.float32), coupling.astype(jnp.float32), precision=lax.Precision.HIGHEST, preferred_element_type=jnp.float32)
    r_factor = upper / jnp.sqrt(jnp.float32(NROWS))
    return (r_factor, residual)
```

```python
import functools
import math

import jax
import jax.numpy as jnp
from jax import lax
from jax.experimental import pallas as pl
from jax.experimental.pallas import tpu as pltpu
from jax.sharding import Mesh, PartitionSpec as P

HI = lax.Precision.HIGHEST
B = 512
NB = 128

def sub_row(v, j):
    return jnp.broadcast_to(v[j:j + 1, :], v.shape)

def factor_block(get, put_r, put_inv):
    sub = lax.broadcasted_iota(jnp.int32, (8, NB), 0)
    lane = lax.broadcasted_iota(jnp.int32, (8, NB), 1)
    a = [get(t) for t in range(NB // 8)]
    y = [jnp.where(lane == sub + 8 * t, 1.0, 0.0).astype(jnp.float32) for t in range(NB // 8)]
    for s in range(NB // 8):
        k = 8 * s
        av, yv = a[s], y[s]
        cols = [jnp.broadcast_to(av[:, k + j:k + j + 1], (8, NB)) for j in range(8)]
        rows_r = jnp.zeros((8, NB), jnp.float32)
        rows_y = jnp.zeros((8, NB), jnp.float32)
        for j in range(8):
            here = sub == j
            d = sub_row(cols[j], j)
            rs = lax.rsqrt(d)
            inv = rs * rs
            ra, ry = sub_row(av, j), sub_row(yv, j)
            rows_r = jnp.where(here, ra * rs, rows_r)
            rows_y = jnp.where(here, ry * rs, rows_y)
            av = jnp.where(here, ra * inv, av - (cols[j] * ra) * inv)
            yv = jnp.where(here, ry * inv, yv - (cols[j] * ry) * inv)
            for m in range(j + 1, 8):
                cm = sub_row(cols[m], j)
                cols[m] = jnp.where(here, cm * inv, cols[m] - (cols[j] * cm) * inv)
        put_r(s, rows_r)
        put_inv(s, rows_y)
        va = [sub_row(av, j) for j in range(8)]
        vy = [sub_row(yv, j) for j in range(8)]
        for t in range(s + 1, NB // 8):
            at, yt = a[t], y[t]
            lc = [jnp.broadcast_to(at[:, k + j:k + j + 1], (8, NB)) for j in range(8)]
            pa = [lc[j] * va[j] for j in range(8)]
            py = [lc[j] * vy[j] for j in range(8)]
            tree = lambda p: ((p[0] + p[1]) + (p[2] + p[3])) + ((p[4] + p[5]) + (p[6] + p[7]))
            a[t] = at - tree(pa)
            y[t] = yt - tree(py)

def chol_kernel(scale, lo_ref, hi_ref, r_ref, m_ref, aug, inv):
    h = B // 2
    aug[0:h, 0:384] = lo_ref[...]
    aug[0:h, 384:B] = hi_ref[:, 0:128]
    aug[h:B, 0:h] = jnp.zeros((h, h), jnp.float32)
    aug[h:B, h:B] = hi_ref[:, 128:384]
    ri = lax.broadcasted_iota(jnp.int32, (B, B), 0)
    ci = lax.broadcasted_iota(jnp.int32, (B, B), 1)
    aug[:, B:2 * B] = jnp.where(ri == ci, 1.0, 0.0).astype(jnp.float32)
    row = lax.broadcasted_iota(jnp.int32, (NB, B), 0)
    col = lax.broadcasted_iota(jnp.int32, (NB, B), 1)

    def block(b, _):
        at = pl.multiple_of(b * NB, NB)
        def get(t):
            return aug[pl.ds(pl.multiple_of(at + 8 * t, 8), 8), pl.ds(at, NB)]
        def put_inv(s, v):
            inv[8 * s:8 * s + 8, :] = v
        diag = []
        def put_r(s, v):
            inv[NB + 8 * s:NB + 8 * s + 8, :] = v
        factor_block(get, put_r, put_inv)
        rows = jnp.dot(inv[0:NB, :], aug[pl.ds(at, NB), :], precision=HI, preferred_element_type=jnp.float32)
        aug[pl.ds(at, NB), :] = rows
        m_ref[pl.ds(at, NB), :] = rows[:, B:]
        r_ref[pl.ds(at, NB), :] = jnp.where(col > row + at, rows[:, :B], 0.0) * scale
        dr = inv[NB:2 * NB, :]
        r2 = lax.broadcasted_iota(jnp.int32, (NB, NB), 0)
        c2 = lax.broadcasted_iota(jnp.int32, (NB, NB), 1)
        r_ref[pl.ds(at, NB), pl.ds(at, NB)] = jnp.where(c2 >= r2, dr, 0.0) * scale
        for i in range(1, B // NB):
            @pl.when(i > b)
            def _():
                left = aug[pl.ds(at, NB), i * NB:(i + 1) * NB]
                upd = lax.dot_general(left, aug[pl.ds(at, NB), :], (((0,), (0,)), ((), ())), precision=HI, preferred_element_type=jnp.float32)
                aug[i * NB:(i + 1) * NB, :] -= upd
        return 0
    lax.fori_loop(0, B // NB, block, 0)

def factor(lo, hi, total_rows):
    f = jax.ShapeDtypeStruct((B, B), jnp.float32)
    return pl.pallas_call(
        functools.partial(chol_kernel, 1.0 / math.sqrt(total_rows)),
        out_shape=(f, f),
        in_specs=[pl.BlockSpec(memory_space=pltpu.VMEM)] * 2,
        out_specs=(pl.BlockSpec(memory_space=pltpu.VMEM),) * 2,
        scratch_shapes=[pltpu.VMEM((B, 2 * B), jnp.float32), pltpu.VMEM((2 * NB, NB), jnp.float32)],
        name="factor",
    )(lo, hi)


def dot(a, b, dims):
    return lax.dot_general(a, b, (dims, ((), ())), precision=HI, preferred_element_type=jnp.float32)


def spread(own, axes, parts):
    copies = jnp.broadcast_to(own[None], (parts,) + own.shape)
    return lax.all_to_all(copies, axes, 0, 0, tiled=True)


def gather_panel(panel):
    return lax.all_gather(panel, "z", axis=0, tiled=True)


def per_device(panel, trailing):
    axes, plane = ("x", "y", "z"), ("x", "y")
    everyone, ring = lax.axis_size(axes), lax.axis_size(plane)
    total_rows = panel.shape[0] * everyone * 2
    core = lax.axis_index("c")
    first = core == 0
    swap = [(0, 1), (1, 0)]
    h = B // 2

    pair = jnp.concatenate([panel, lax.ppermute(panel, "c", swap)], axis=0)
    top = dot(pair[:, :h], pair, ((0,), (0,)))
    low = dot(pair[:, h:], pair[:, h:], ((0,), (0,)))
    half = jnp.where(first, top[:, :384], jnp.concatenate([top[:, 384:], low], axis=1))
    pieces = lax.all_to_all(half.reshape(everyone, -1, 128), axes, 0, 0, tiled=True)
    mine = spread(jnp.sum(pieces, axis=0), axes, everyone).reshape(h, 384)
    other = lax.ppermute(mine, "c", swap)
    upper, inverse = factor(
        jnp.where(first, mine, other), jnp.where(first, other, mine), total_rows
    )

    block = gather_panel(panel)
    coupling = dot(block, trailing, ((0,), (0,)))
    keep = lax.dynamic_slice(coupling, (core * h, 0), (h, coupling.shape[1]))
    give = lax.dynamic_slice(coupling, ((1 - core) * h, 0), (h, coupling.shape[1]))
    keep = keep + lax.ppermute(give, "c", swap)
    pieces = lax.all_to_all(keep.reshape(ring, h // ring, -1), plane, 0, 0, tiled=True)
    mine = spread(jnp.sum(pieces, axis=0), plane, ring).reshape(h, -1)
    other = lax.ppermute(mine, "c", swap)

    basis = dot(block, inverse, ((1,), (1,)))
    weights = dot(basis, inverse, ((1,), (0,)))
    rows = block.shape[0]
    near = lax.dynamic_slice(weights, (0, core * h), (rows, h))
    far = lax.dynamic_slice(weights, (0, (1 - core) * h), (rows, h))
    residual = trailing - dot(near, mine, ((1,), (0,))) - dot(far, other, ((1,), (0,)))
    return (upper, residual)


def solution(mesh):
    row, col = mesh.devices.shape
    y = 8 if row == 64 else 2
    fine = Mesh(mesh.devices.reshape(row // (2 * y), y, 2, col), ("x", "y", "c", "z"))
    row_axes = ("x", "y", "c")
    return jax.shard_map(
        per_device,
        mesh=fine,
        in_specs=(P(row_axes + ("z",), None), P(row_axes, "z")),
        out_specs=(P(), P(row_axes, "z")),
        check_vma=False,
    )
```

```python
import functools
import math

import jax
import jax.numpy as jnp
from jax import lax
from jax.experimental import pallas as pl
from jax.experimental.pallas import tpu as pltpu
from jax.sharding import Mesh, PartitionSpec as P


HI = lax.Precision.HIGHEST
B = 512
NB = 128
F32 = jnp.float32


def gram_kernel(which, a_ref, b_ref, out_ref):
    h = B // 2

    def prod(rows, cols):
        total = None
        for ref in (a_ref, b_ref):
            term = lax.dot_general(
                ref[:, rows], ref[:, cols], (((0,), (0,)), ((), ())), precision=HI, preferred_element_type=F32
            )
            total = term if total is None else total + term
        return total

    def put(j, v):
        for i in range(v.shape[1] // NB):
            out_ref[:, j + i, :] = v[:, i * NB:(i + 1) * NB]

    @pl.when(which[0] == 0)
    def _():
        put(0, prod(slice(0, h), slice(0, 384)))

    @pl.when(which[0] != 0)
    def _():
        put(0, prod(slice(0, h), slice(384, B)))
        put(1, prod(slice(h, B), slice(h, B)))


def sub_row(v, j):
    return jnp.broadcast_to(v[j:j + 1, :], v.shape)


def factor_block(get, put_r, put_inv):
    sub = lax.broadcasted_iota(jnp.int32, (8, NB), 0)
    lane = lax.broadcasted_iota(jnp.int32, (8, NB), 1)
    a = [get(t) for t in range(NB // 8)]
    y = [jnp.where(lane == sub + 8 * t, 1.0, 0.0).astype(jnp.float32) for t in range(NB // 8)]
    for s in range(NB // 8):
        k = 8 * s
        av, yv = a[s], y[s]
        cols = [jnp.broadcast_to(av[:, k + j:k + j + 1], (8, NB)) for j in range(8)]
        rows_r = jnp.zeros((8, NB), jnp.float32)
        rows_y = jnp.zeros((8, NB), jnp.float32)
        for j in range(8):
            here = sub == j
            d = sub_row(cols[j], j)
            rs = lax.rsqrt(d)
            inv = rs * rs
            ra, ry = sub_row(av, j), sub_row(yv, j)
            rows_r = jnp.where(here, ra * rs, rows_r)
            rows_y = jnp.where(here, ry * rs, rows_y)
            av = jnp.where(here, ra * inv, av - (cols[j] * ra) * inv)
            yv = jnp.where(here, ry * inv, yv - (cols[j] * ry) * inv)
            for m in range(j + 1, 8):
                cm = sub_row(cols[m], j)
                cols[m] = jnp.where(here, cm * inv, cols[m] - (cols[j] * cm) * inv)
        put_r(s, rows_r)
        put_inv(s, rows_y)
        va = [sub_row(av, j) for j in range(8)]
        vy = [sub_row(yv, j) for j in range(8)]
        for t in range(s + 1, NB // 8):
            at, yt = a[t], y[t]
            lc = [jnp.broadcast_to(at[:, k + j:k + j + 1], (8, NB)) for j in range(8)]
            pa = [lc[j] * va[j] for j in range(8)]
            py = [lc[j] * vy[j] for j in range(8)]
            tree = lambda p: ((p[0] + p[1]) + (p[2] + p[3])) + ((p[4] + p[5]) + (p[6] + p[7]))
            a[t] = at - tree(pa)
            y[t] = yt - tree(py)


def run_block(aug, inv, at, width, blocks, r_ref, m_ref, scale, a_from):
    b = at // NB

    def get(t):
        return aug[pl.ds(pl.multiple_of(at + 8 * t, 8), 8), pl.ds(at, NB)]

    def put_inv(s, v):
        inv[8 * s:8 * s + 8, :] = v

    def put_r(s, v):
        inv[NB + 8 * s:NB + 8 * s + 8, :] = v

    factor_block(get, put_r, put_inv)
    rows = jnp.dot(inv[0:NB, :], aug[pl.ds(at, NB), :], precision=HI, preferred_element_type=F32)
    aug[pl.ds(at, NB), :] = rows
    row = lax.broadcasted_iota(jnp.int32, (NB, width), 0)
    col = lax.broadcasted_iota(jnp.int32, (NB, width), 1)
    m_ref(at, rows[:, width:])
    r_ref(at, jnp.where(col > row + at, rows[:, :width], 0.0) * scale)
    r2 = lax.broadcasted_iota(jnp.int32, (NB, NB), 0)
    c2 = lax.broadcasted_iota(jnp.int32, (NB, NB), 1)
    a_from(at, jnp.where(c2 >= r2, inv[NB:2 * NB, :], 0.0) * scale)
    for i in range(1, blocks):
        @pl.when(i > b)
        def _():
            left = aug[pl.ds(at, NB), i * NB:(i + 1) * NB]
            upd = lax.dot_general(
                left, aug[pl.ds(at, NB), :], (((0,), (0,)), ((), ())), precision=HI, preferred_element_type=F32
            )
            aug[i * NB:(i + 1) * NB, :] -= upd


def top_kernel(scale, which, mine_ref, other_ref, r_out, m_out, tail_out, aug, inv):
    h = B // 2

    def load(lo, hi):
        for i in range(3):
            aug[0:h, i * NB:(i + 1) * NB] = lo[:, i, :]
        aug[0:h, 384:B] = hi[:, 0, :]
        for i in range(2):
            aug[h:B, h + i * NB:h + (i + 1) * NB] = hi[:, 1 + i, :]

    @pl.when(which[0] == 0)
    def _():
        load(mine_ref, other_ref)

    @pl.when(which[0] != 0)
    def _():
        load(other_ref, mine_ref)

    aug[h:B, 0:h] = jnp.zeros((h, h), F32)
    ri = lax.broadcasted_iota(jnp.int32, (h, h), 0)
    ci = lax.broadcasted_iota(jnp.int32, (h, h), 1)
    aug[0:h, B:] = jnp.where(ri == ci, 1.0, 0.0).astype(F32)
    aug[h:B, B:] = jnp.zeros((h, h), F32)

    def block(b, _):
        at = pl.multiple_of(b * NB, NB)

        def put_m(at, v):
            m_out[pl.ds(at, NB), :] = v

        def put_r(at, v):
            r_out[pl.ds(at, NB), :] = v

        def put_d(at, v):
            r_out[pl.ds(at, NB), pl.ds(at, NB)] = v

        run_block(aug, inv, at, B, B // NB, put_r, put_m, scale, put_d)
        return 0

    lax.fori_loop(0, 2, block, 0)
    tail_out[...] = aug[h:B, h:]


def low_kernel(scale, top_ref, mtop_ref, tail_ref, r_out, m_out, aug, inv):
    h = B // 2
    r_out[0:h, :] = top_ref[...]
    r_out[h:B, 0:h] = jnp.zeros((h, h), F32)
    m_out[0:h, 0:h] = mtop_ref[...]
    m_out[0:h, h:B] = jnp.zeros((h, h), F32)
    aug[:, 0:B] = tail_ref[...]
    ri = lax.broadcasted_iota(jnp.int32, (h, h), 0)
    ci = lax.broadcasted_iota(jnp.int32, (h, h), 1)
    aug[:, B:] = jnp.where(ri == ci, 1.0, 0.0).astype(F32)

    def block(b, _):
        at = pl.multiple_of(b * NB, NB)

        def put_m(at, v):
            m_out[pl.ds(at + h, NB), :] = v

        def put_r(at, v):
            r_out[pl.ds(at + h, NB), h:B] = v

        def put_d(at, v):
            r_out[pl.ds(at + h, NB), pl.ds(at + h, NB)] = v

        run_block(aug, inv, at, h, 2, put_r, put_m, scale, put_d)
        return 0

    lax.fori_loop(0, 2, block, 0)


VM = pl.BlockSpec(memory_space=pltpu.VMEM)
SM = pl.BlockSpec(memory_space=pltpu.SMEM)


def gram(which, panel, partner):
    return pl.pallas_call(
        gram_kernel,
        out_shape=jax.ShapeDtypeStruct((B // 2, 3, NB), F32),
        in_specs=[SM, VM, VM],
        out_specs=VM,
        name="gram",
    )(which, panel, partner)


def factor_top(which, mine, other, total_rows):
    h = B // 2
    return pl.pallas_call(
        functools.partial(top_kernel, 1.0 / math.sqrt(total_rows)),
        out_shape=[jax.ShapeDtypeStruct(s, F32) for s in ((h, B), (h, h), (h, B))],
        in_specs=[SM, VM, VM],
        out_specs=[VM] * 3,
        scratch_shapes=[pltpu.VMEM((B, B + h), F32), pltpu.VMEM((2 * NB, NB), F32)],
        name="factor_top",
    )(which, mine, other)


def factor_low(top, top_inverse, tail, total_rows):
    h = B // 2
    return pl.pallas_call(
        functools.partial(low_kernel, 1.0 / math.sqrt(total_rows)),
        out_shape=[jax.ShapeDtypeStruct((B, B), F32)] * 2,
        in_specs=[VM] * 3,
        out_specs=[VM] * 2,
        scratch_shapes=[pltpu.VMEM((h, h + B), F32), pltpu.VMEM((2 * NB, NB), F32)],
        name="factor_low",
    )(top, top_inverse, tail)


def dot(a, b, dims, precision=HI):
    return lax.dot_general(a, b, (dims, ((), ())), precision=precision, preferred_element_type=jnp.float32)


def spread(own, axes, parts):
    copies = jnp.broadcast_to(own[None], (parts,) + own.shape)
    return lax.all_to_all(copies, axes, 0, 0, tiled=True)


def per_device(panel, trailing):
    high = lax.Precision.HIGH
    axes, plane = ("x", "y", "z"), ("x", "y")
    everyone, ring, depth = lax.axis_size(axes), lax.axis_size(plane), lax.axis_size("z")
    total_rows = panel.shape[0] * everyone * 2
    core = lax.axis_index("c")
    place = lax.axis_index("z")
    swap = [(0, 1), (1, 0)]
    h = B // 2
    each = panel.shape[0]
    which = jnp.full((1,), core, jnp.int32)

    block = jnp.zeros((depth * each, B), jnp.float32)
    block = lax.dynamic_update_slice(block, panel, (place * each, 0))
    forth = back = panel
    for k in range(1, depth // 2 + 1):
        forth = lax.ppermute(forth, "z", [(i, (i + 1) % depth) for i in range(depth)])
        block = lax.dynamic_update_slice(block, forth, ((place + depth - k) % depth * each, 0))
        if k < depth - k:
            back = lax.ppermute(back, "z", [(i, (i - 1) % depth) for i in range(depth)])
            block = lax.dynamic_update_slice(block, back, ((place + k) % depth * each, 0))

    partner = lax.ppermute(panel, "c", swap)
    half = gram(which, panel, partner)
    pieces = lax.all_to_all(half.reshape((everyone, -1) + half.shape[2:]) if everyone != h else half, axes, 0, 0, tiled=True)
    own = jnp.sum(pieces, axis=0)
    mine = spread(own, axes, everyone).reshape(half.shape)
    other = lax.ppermute(mine, "c", swap)
    top, top_inverse, tail = factor_top(which, mine, other, total_rows)
    upper, inverse = factor_low(top, top_inverse, tail, total_rows)

    give = dot(lax.dynamic_slice(block, (0, (1 - core) * h), (depth * each, h)), trailing, ((0,), (0,)), high)
    got = lax.ppermute(give, "c", swap)
    keep = dot(lax.dynamic_slice(block, (0, core * h), (depth * each, h)), trailing, ((0,), (0,)), high)
    pieces = lax.all_to_all((keep + got).reshape(ring, h // ring, -1), plane, 0, 0, tiled=True)
    own = jnp.sum(pieces, axis=0)
    near = spread(own, plane, ring).reshape(h, -1)
    far = lax.ppermute(near, "c", swap)

    ginv = dot(inverse, inverse, ((0,), (0,)))
    weights = dot(lax.dynamic_slice(ginv, (core * h, 0), (h, B)), near, ((0,), (0,)))
    weights = weights + dot(lax.dynamic_slice(ginv, ((1 - core) * h, 0), (h, B)), far, ((0,), (0,)))
    residual = trailing - dot(block, weights, ((1,), (0,)), high)
    return (upper, residual)


def solution(mesh):
    row, col = mesh.devices.shape
    y = 8 if row == 64 else 2
    fine = Mesh(mesh.devices.reshape(row // (2 * y), y, 2, col), ("x", "y", "c", "z"))
    row_axes = ("x", "y", "c")
    return jax.shard_map(
        per_device,
        mesh=fine,
        in_specs=(P(row_axes + ("z",), None), P(row_axes, "z")),
        out_specs=(P(), P(row_axes, "z")),
        check_vma=False,
    )
```

```python
import functools
import math

import jax
import jax.numpy as jnp
from jax import lax
from jax.experimental import pallas as pl
from jax.experimental.pallas import tpu as pltpu
from jax.sharding import Mesh, PartitionSpec as P


HI = lax.Precision.HIGHEST
B = 512
NB = 128
F32 = jnp.float32


def gram_kernel(which, a_ref, b_ref, out_ref):
    h = B // 2

    def prod(rows, cols):
        total = None
        for ref in (a_ref, b_ref):
            term = lax.dot_general(
                ref[:, rows], ref[:, cols], (((0,), (0,)), ((), ())), precision=HI, preferred_element_type=F32
            )
            total = term if total is None else total + term
        return total

    def put(j, v):
        for i in range(v.shape[1] // NB):
            tiles = v[:, i * NB:(i + 1) * NB].reshape(h // 8, 8, NB)
            out_ref[:, 8 * (j + i):8 * (j + i + 1), :] = tiles

    @pl.when(which[0] == 0)
    def _():
        put(0, prod(slice(0, h), slice(0, 384)))

    @pl.when(which[0] != 0)
    def _():
        put(0, prod(slice(0, h), slice(384, B)))
        put(1, prod(slice(h, B), slice(h, B)))


def sub_row(v, j):
    return jnp.broadcast_to(v[j:j + 1, :], v.shape)


def factor_block(get, put_r, put_inv):
    sub = lax.broadcasted_iota(jnp.int32, (8, NB), 0)
    lane = lax.broadcasted_iota(jnp.int32, (8, NB), 1)
    a = [get(t) for t in range(NB // 8)]
    y = [jnp.where(lane == sub + 8 * t, 1.0, 0.0).astype(jnp.float32) for t in range(NB // 8)]
    for s in range(NB // 8):
        k = 8 * s
        av, yv = a[s], y[s]
        cols = [jnp.broadcast_to(av[:, k + j:k + j + 1], (8, NB)) for j in range(8)]
        rows_r = jnp.zeros((8, NB), jnp.float32)
        rows_y = jnp.zeros((8, NB), jnp.float32)
        for j in range(8):
            here = sub == j
            d = sub_row(cols[j], j)
            rs = lax.rsqrt(d)
            inv = rs * rs
            ra, ry = sub_row(av, j), sub_row(yv, j)
            rows_r = jnp.where(here, ra * rs, rows_r)
            rows_y = jnp.where(here, ry * rs, rows_y)
            av = jnp.where(here, ra * inv, av - (cols[j] * ra) * inv)
            yv = jnp.where(here, ry * inv, yv - (cols[j] * ry) * inv)
            for m in range(j + 1, 8):
                cm = sub_row(cols[m], j)
                cols[m] = jnp.where(here, cm * inv, cols[m] - (cols[j] * cm) * inv)
        put_r(s, rows_r)
        put_inv(s, rows_y)
        va = [sub_row(av, j) for j in range(8)]
        vy = [sub_row(yv, j) for j in range(8)]
        for t in range(s + 1, NB // 8):
            at, yt = a[t], y[t]
            lc = [jnp.broadcast_to(at[:, k + j:k + j + 1], (8, NB)) for j in range(8)]
            pa = [lc[j] * va[j] for j in range(8)]
            py = [lc[j] * vy[j] for j in range(8)]
            tree = lambda p: ((p[0] + p[1]) + (p[2] + p[3])) + ((p[4] + p[5]) + (p[6] + p[7]))
            a[t] = at - tree(pa)
            y[t] = yt - tree(py)


def run_block(aug, inv, at, width, blocks, r_ref, m_ref, scale, a_from):
    b = at // NB

    def get(t):
        return aug[pl.ds(pl.multiple_of(at + 8 * t, 8), 8), pl.ds(at, NB)]

    def put_inv(s, v):
        inv[8 * s:8 * s + 8, :] = v

    def put_r(s, v):
        inv[NB + 8 * s:NB + 8 * s + 8, :] = v

    factor_block(get, put_r, put_inv)
    rows = jnp.dot(inv[0:NB, :], aug[pl.ds(at, NB), :], precision=HI, preferred_element_type=F32)
    aug[pl.ds(at, NB), :] = rows
    row = lax.broadcasted_iota(jnp.int32, (NB, width), 0)
    col = lax.broadcasted_iota(jnp.int32, (NB, width), 1)
    m_ref(at, rows[:, width:])
    r_ref(at, jnp.where(col > row + at, rows[:, :width], 0.0) * scale)
    r2 = lax.broadcasted_iota(jnp.int32, (NB, NB), 0)
    c2 = lax.broadcasted_iota(jnp.int32, (NB, NB), 1)
    a_from(at, jnp.where(c2 >= r2, inv[NB:2 * NB, :], 0.0) * scale)
    for i in range(1, blocks):
        @pl.when(i > b)
        def _():
            left = aug[pl.ds(at, NB), i * NB:(i + 1) * NB]
            upd = lax.dot_general(
                left, aug[pl.ds(at, NB), :], (((0,), (0,)), ((), ())), precision=HI, preferred_element_type=F32
            )
            aug[i * NB:(i + 1) * NB, :] -= upd


def top_kernel(scale, which, mine_ref, other_ref, r_out, m_out, tail_out, aug, inv):
    h = B // 2

    def load(lo, hi):
        def tiles(ref, i):
            return ref[:, 8 * i:8 * i + 8, :].reshape(h, NB)

        for i in range(3):
            aug[0:h, i * NB:(i + 1) * NB] = tiles(lo, i)
        aug[0:h, 384:B] = tiles(hi, 0)
        for i in range(2):
            aug[h:B, h + i * NB:h + (i + 1) * NB] = tiles(hi, 1 + i)

    @pl.when(which[0] == 0)
    def _():
        load(mine_ref, other_ref)

    @pl.when(which[0] != 0)
    def _():
        load(other_ref, mine_ref)

    aug[h:B, 0:h] = jnp.zeros((h, h), F32)
    ri = lax.broadcasted_iota(jnp.int32, (h, h), 0)
    ci = lax.broadcasted_iota(jnp.int32, (h, h), 1)
    aug[0:h, B:] = jnp.where(ri == ci, 1.0, 0.0).astype(F32)
    aug[h:B, B:] = jnp.zeros((h, h), F32)

    def block(b, _):
        at = pl.multiple_of(b * NB, NB)

        def put_m(at, v):
            m_out[pl.ds(at, NB), :] = v

        def put_r(at, v):
            r_out[pl.ds(at, NB), :] = v

        def put_d(at, v):
            r_out[pl.ds(at, NB), pl.ds(at, NB)] = v

        run_block(aug, inv, at, B, B // NB, put_r, put_m, scale, put_d)
        return 0

    lax.fori_loop(0, 2, block, 0)
    tail_out[...] = aug[h:B, h:]


def low_kernel(scale, top_ref, mtop_ref, tail_ref, r_out, m_out, aug, inv):
    h = B // 2
    r_out[0:h, :] = top_ref[...]
    r_out[h:B, 0:h] = jnp.zeros((h, h), F32)
    m_out[0:h, 0:h] = mtop_ref[...]
    m_out[0:h, h:B] = jnp.zeros((h, h), F32)
    aug[:, 0:B] = tail_ref[...]
    ri = lax.broadcasted_iota(jnp.int32, (h, h), 0)
    ci = lax.broadcasted_iota(jnp.int32, (h, h), 1)
    aug[:, B:] = jnp.where(ri == ci, 1.0, 0.0).astype(F32)

    def block(b, _):
        at = pl.multiple_of(b * NB, NB)

        def put_m(at, v):
            m_out[pl.ds(at + h, NB), :] = v

        def put_r(at, v):
            r_out[pl.ds(at + h, NB), h:B] = v

        def put_d(at, v):
            r_out[pl.ds(at + h, NB), pl.ds(at + h, NB)] = v

        run_block(aug, inv, at, h, 2, put_r, put_m, scale, put_d)
        return 0

    lax.fori_loop(0, 2, block, 0)


VM = pl.BlockSpec(memory_space=pltpu.VMEM)
SM = pl.BlockSpec(memory_space=pltpu.SMEM)


def gram(which, panel, partner):
    return pl.pallas_call(
        gram_kernel,
        out_shape=jax.ShapeDtypeStruct((B // 16, 24, NB), F32),
        in_specs=[SM, VM, VM],
        out_specs=VM,
        name="gram",
    )(which, panel, partner)


def factor_top(which, mine, other, total_rows):
    h = B // 2
    return pl.pallas_call(
        functools.partial(top_kernel, 1.0 / math.sqrt(total_rows)),
        out_shape=[jax.ShapeDtypeStruct(s, F32) for s in ((h, B), (h, h), (h, B))],
        in_specs=[SM, VM, VM],
        out_specs=[VM] * 3,
        scratch_shapes=[pltpu.VMEM((B, B + h), F32), pltpu.VMEM((2 * NB, NB), F32)],
        name="factor_top",
    )(which, mine, other)


def factor_low(top, top_inverse, tail, total_rows):
    h = B // 2
    return pl.pallas_call(
        functools.partial(low_kernel, 1.0 / math.sqrt(total_rows)),
        out_shape=[jax.ShapeDtypeStruct((B, B), F32)] * 2,
        in_specs=[VM] * 3,
        out_specs=[VM] * 2,
        scratch_shapes=[pltpu.VMEM((h, h + B), F32), pltpu.VMEM((2 * NB, NB), F32)],
        name="factor_low",
    )(top, top_inverse, tail)


def dot(a, b, dims, precision=HI):
    return lax.dot_general(a, b, (dims, ((), ())), precision=precision, preferred_element_type=jnp.float32)


def spread(own, axes, parts):
    copies = jnp.broadcast_to(own[None], (parts,) + own.shape)
    return lax.all_to_all(copies, axes, 0, 0, tiled=True)


def per_device(panel, trailing):
    high = lax.Precision.HIGH
    plane = ("x", "y")
    ring, depth = lax.axis_size(plane), lax.axis_size("z")
    total_rows = panel.shape[0] * ring * depth * 2
    core = lax.axis_index("c")
    place = lax.axis_index("z")
    swap = [(0, 1), (1, 0)]
    h = B // 2
    each = panel.shape[0]
    which = jnp.full((1,), core, jnp.int32)

    block = jnp.zeros((depth * each, B), jnp.float32)
    block = lax.dynamic_update_slice(block, panel, (place * each, 0))
    forth = back = panel
    for k in range(1, depth // 2 + 1):
        forth = lax.ppermute(forth, "z", [(i, (i + 1) % depth) for i in range(depth)])
        block = lax.dynamic_update_slice(block, forth, ((place + depth - k) % depth * each, 0))
        if k < depth - k:
            back = lax.ppermute(back, "z", [(i, (i - 1) % depth) for i in range(depth)])
            block = lax.dynamic_update_slice(block, back, ((place + k) % depth * each, 0))

    partner = lax.ppermute(panel, "c", swap)
    half = gram(which, panel, partner)
    pieces = lax.all_to_all(half.reshape(ring, -1, NB), plane, 0, 0, tiled=True)
    own = jnp.sum(pieces, axis=0)
    own = jnp.sum(spread(own, "z", depth).reshape((depth,) + own.shape), axis=0)
    mine = spread(own, plane, ring).reshape(half.shape)
    other = lax.ppermute(mine, "c", swap)
    top, top_inverse, tail = factor_top(which, mine, other, total_rows)
    upper, inverse = factor_low(top, top_inverse, tail, total_rows)

    give = dot(lax.dynamic_slice(block, (0, (1 - core) * h), (depth * each, h)), trailing, ((0,), (0,)), high)
    got = lax.ppermute(give, "c", swap)
    keep = dot(lax.dynamic_slice(block, (0, core * h), (depth * each, h)), trailing, ((0,), (0,)), high)
    pieces = lax.all_to_all((keep + got).reshape(ring, h // ring, -1), plane, 0, 0, tiled=True)
    own = jnp.sum(pieces, axis=0)
    near = spread(own, plane, ring).reshape(h, -1)
    far = lax.ppermute(near, "c", swap)

    ginv = dot(inverse, inverse, ((0,), (0,)))
    weights = dot(lax.dynamic_slice(ginv, (core * h, 0), (h, B)), near, ((0,), (0,)))
    weights = weights + dot(lax.dynamic_slice(ginv, ((1 - core) * h, 0), (h, B)), far, ((0,), (0,)))
    residual = trailing - dot(block, weights, ((1,), (0,)), high)
    return (upper, residual)


def solution(mesh):
    row, col = mesh.devices.shape
    y = 8 if row == 64 else 2
    fine = Mesh(mesh.devices.reshape(row // (2 * y), y, 2, col), ("x", "y", "c", "z"))
    row_axes = ("x", "y", "c")
    return jax.shard_map(
        per_device,
        mesh=fine,
        in_specs=(P(row_axes + ("z",), None), P(row_axes, "z")),
        out_specs=(P(), P(row_axes, "z")),
        check_vma=False,
    )
```

```python
import functools
import math

import jax
import jax.numpy as jnp
from jax import lax
from jax.experimental import pallas as pl
from jax.experimental.pallas import tpu as pltpu
from jax.sharding import Mesh, PartitionSpec as P


HI = lax.Precision.HIGHEST
B = 512
NB = 128
F32 = jnp.float32


def gram_kernel(which, a_ref, b_ref, out_ref):
    h = B // 2

    def prod(rows, cols):
        total = None
        for ref in (a_ref, b_ref):
            term = lax.dot_general(
                ref[:, rows], ref[:, cols], (((0,), (0,)), ((), ())), precision=HI, preferred_element_type=F32
            )
            total = term if total is None else total + term
        return total

    def put(j, v):
        for i in range(v.shape[1] // NB):
            tiles = v[:, i * NB:(i + 1) * NB].reshape(h // 8, 8, NB)
            out_ref[:, 8 * (j + i):8 * (j + i + 1), :] = tiles

    @pl.when(which[0] == 0)
    def _():
        put(0, prod(slice(0, h), slice(0, 384)))

    @pl.when(which[0] != 0)
    def _():
        put(0, prod(slice(0, h), slice(384, B)))
        put(1, prod(slice(h, B), slice(h, B)))


def sub_row(v, j):
    return jnp.broadcast_to(v[j:j + 1, :], v.shape)


def tree(p):
    return ((p[0] + p[1]) + (p[2] + p[3])) + ((p[4] + p[5]) + (p[6] + p[7]))


def solve_strip(a, y, cols, sub):
    rows_r = rows_y = jnp.zeros_like(a)
    for j in range(0, 8, 2):
        h0, h1 = sub == j, sub == j + 1
        c0, c1 = cols[j], cols[j + 1]
        d0, b, d1 = sub_row(c0, j), sub_row(c1, j), sub_row(c1, j + 1)
        det = d0 * d1 - b * b
        rdet = 1.0 / det
        r0 = lax.rsqrt(d0)
        r1 = lax.rsqrt(det) * (d0 * r0)
        g = b * (r0 * r0)
        e0 = jnp.where(h0, -d1, jnp.where(h1, b, c0 * d1 - c1 * b))
        e1 = jnp.where(h0, b, jnp.where(h1, -d0, c1 * d0 - c0 * b))
        pair = h0 | h1

        def apply(v):
            v0, v1 = sub_row(v, j), sub_row(v, j + 1)
            return jnp.where(pair, 0.0, v) - (e0 * v0 + e1 * v1) * rdet, v0, v1

        a, a0, a1 = apply(a)
        y, y0, y1 = apply(y)
        rows_r = jnp.where(h0, a0 * r0, jnp.where(h1, (a1 - g * a0) * r1, rows_r))
        rows_y = jnp.where(h0, y0 * r0, jnp.where(h1, (y1 - g * y0) * r1, rows_y))
        for m in range(j + 2, 8):
            cols[m] = apply(cols[m])[0]
    return a, y, rows_r, rows_y


def factor_block(aug, inv, at):
    sub = lax.broadcasted_iota(jnp.int32, (8, NB), 0)
    lane = lax.broadcasted_iota(jnp.int32, (8, NB), 1)
    strips = range(NB // 8)
    a = [aug[at + 8 * t:at + 8 * t + 8, at:at + NB] for t in strips]
    y = [jnp.where(lane == sub + 8 * t, 1.0, 0.0).astype(F32) for t in strips]
    for s in strips:
        lanes = [slice(8 * s + j, 8 * s + j + 1) for j in range(8)]
        cols = [jnp.broadcast_to(a[s][:, c], (8, NB)) for c in lanes]
        av, yv, rows_r, rows_y = solve_strip(a[s], y[s], cols, sub)
        inv[8 * s:8 * s + 8, :] = rows_y
        inv[NB + 8 * s:NB + 8 * s + 8, :] = rows_r
        va = [sub_row(av, j) for j in range(8)]
        vy = [sub_row(yv, j) for j in range(8)]
        for t in range(s + 1, NB // 8):
            left = [jnp.broadcast_to(a[t][:, c], (8, NB)) for c in lanes]
            a[t] = a[t] - tree([u * v for u, v in zip(left, va)])
            y[t] = y[t] - tree([u * v for u, v in zip(left, vy)])


def run_block(aug, inv, at, width, done):
    factor_block(aug, inv, at)
    rows = slice(at, at + NB)
    end = width + done
    aug[rows, at + NB:end] = jnp.dot(
        inv[0:NB, :], aug[rows, at + NB:end], precision=HI, preferred_element_type=F32
    )
    aug[rows, end:end + NB] = inv[0:NB, :]
    for low in range(at + NB, width, NB):
        aug[low:low + NB, low:end + NB] -= lax.dot_general(
            aug[rows, low:low + NB], aug[rows, low:end + NB],
            (((0,), (0,)), ((), ())), precision=HI, preferred_element_type=F32,
        )


def triangle(inv):
    r = lax.broadcasted_iota(jnp.int32, (NB, NB), 0)
    c = lax.broadcasted_iota(jnp.int32, (NB, NB), 1)
    return jnp.where(c >= r, inv[NB:2 * NB, :], 0.0)


def top_kernel(scale, which, mine_ref, other_ref, r_out, m_out, tail_out, s_out, aug, inv):
    h = B // 2

    def load(lo, hi):
        def tiles(ref, i):
            return ref[:, 8 * i:8 * i + 8, :].reshape(h, NB)

        for i in range(3):
            aug[0:h, i * NB:(i + 1) * NB] = tiles(lo, i)
        aug[0:h, 384:B] = tiles(hi, 0)
        for i in range(2):
            aug[h:B, h + i * NB:h + (i + 1) * NB] = tiles(hi, 1 + i)

    @pl.when(which[0] == 0)
    def _():
        load(mine_ref, other_ref)

    @pl.when(which[0] != 0)
    def _():
        load(other_ref, mine_ref)

    eye = lax.broadcasted_iota(jnp.int32, (NB, NB), 0) == lax.broadcasted_iota(jnp.int32, (NB, NB), 1)
    col = []
    for at in range(0, B, NB):
        diag = jnp.where(eye, aug[at:at + NB, at:at + NB], 0.0)
        row = jnp.sum(diag, axis=0, keepdims=True)
        s_out[0:1, at:at + NB] = lax.rsqrt(row)
        s_out[1:2, at:at + NB] = row * lax.rsqrt(row) * scale
        col.append(lax.rsqrt(jnp.sum(diag, axis=1, keepdims=True)))
    for b in range(B // NB):
        rows, cols = slice(b * NB, (b + 1) * NB), slice(b * NB, B)
        aug[rows, cols] = aug[rows, cols] * col[b] * s_out[0:1, cols]
    aug[:, B:] = jnp.zeros((B, h), F32)

    for at in (0, NB):
        run_block(aug, inv, at, B, at)
        rows = slice(at, at + NB)
        r_out[rows, at:at + NB] = triangle(inv) * s_out[1:2, at:at + NB]
        r_out[rows, at + NB:B] = aug[rows, at + NB:B] * s_out[1:2, at + NB:B]
        m_out[rows, :] = aug[rows, B:] * s_out[0:1, 0:h]
    r_out[NB:h, 0:NB] = jnp.zeros((NB, NB), F32)
    tail_out[...] = aug[h:B, h:]


def low_kernel(top_ref, mtop_ref, tail_ref, s_ref, r_out, g_out, aug, inv, low):
    h = B // 2
    r_out[0:h, :] = top_ref[...]
    r_out[h:B, 0:h] = jnp.zeros((h, h), F32)
    aug[:, 0:B] = tail_ref[...]
    aug[:, B:] = jnp.zeros((h, h), F32)
    for at in (0, NB):
        run_block(aug, inv, at, h, h + at)
        rows = slice(at, at + NB)
        g = h + at
        r_out[g:g + NB, g:g + NB] = triangle(inv) * s_ref[1:2, g:g + NB]
        if g + NB < B:
            r_out[g:g + NB, g + NB:B] = aug[rows, at + NB:h] * s_ref[1:2, g + NB:B]
        low[rows, :] = aug[rows, h:] * s_ref[0:1, :]
    r_out[B - NB:B, h:B - NB] = jnp.zeros((NB, NB), F32)

    def square(a, b):
        return lax.dot_general(a, b, (((0,), (0,)), ((), ())), precision=HI, preferred_element_type=F32)

    g_out[0:h, 0:h] = square(low[:, 0:h], low[:, 0:h]) + square(mtop_ref[...], mtop_ref[...])
    g_out[h:B, :] = square(low[:, h:B], low[...])
    g_out[0:h, h:B] = square(low[:, 0:h], low[:, h:B])


VM = pl.BlockSpec(memory_space=pltpu.VMEM)
SM = pl.BlockSpec(memory_space=pltpu.SMEM)


def gram(which, panel, partner):
    return pl.pallas_call(
        gram_kernel,
        out_shape=jax.ShapeDtypeStruct((B // 16, 24, NB), F32),
        in_specs=[SM, VM, VM],
        out_specs=VM,
        name="gram",
    )(which, panel, partner)


def factor_top(which, mine, other, total_rows):
    h = B // 2
    return pl.pallas_call(
        functools.partial(top_kernel, 1.0 / math.sqrt(total_rows)),
        out_shape=[jax.ShapeDtypeStruct(s, F32) for s in ((h, B), (h, h), (h, B), (8, B))],
        in_specs=[SM, VM, VM],
        out_specs=[VM] * 4,
        scratch_shapes=[pltpu.VMEM((B, B + h), F32), pltpu.VMEM((2 * NB, NB), F32)],
        name="factor_top",
    )(which, mine, other)


def factor_low(top, top_inverse, tail, scales):
    h = B // 2
    return pl.pallas_call(
        low_kernel,
        out_shape=[jax.ShapeDtypeStruct((B, B), F32)] * 2,
        in_specs=[VM] * 4,
        out_specs=[VM] * 2,
        scratch_shapes=[pltpu.VMEM((h, h + B), F32), pltpu.VMEM((2 * NB, NB), F32), pltpu.VMEM((h, B), F32)],
        name="factor_low",
    )(top, top_inverse, tail, scales)


def dot(a, b, dims, precision=HI):
    return lax.dot_general(a, b, (dims, ((), ())), precision=precision, preferred_element_type=jnp.float32)


def spread(own, axes, parts):
    copies = jnp.broadcast_to(own[None], (parts,) + own.shape)
    return lax.all_to_all(copies, axes, 0, 0, tiled=True)


def per_device(panel, trailing):
    high = lax.Precision.HIGH
    plane = ("x", "y")
    ring, depth = lax.axis_size(plane), lax.axis_size("z")
    total_rows = panel.shape[0] * ring * depth * 2
    core = lax.axis_index("c")
    place = lax.axis_index("z")
    swap = [(0, 1), (1, 0)]
    h = B // 2
    each = panel.shape[0]
    which = jnp.full((1,), core, jnp.int32)

    block = jnp.zeros((depth * each, B), jnp.float32)
    block = lax.dynamic_update_slice(block, panel, (place * each, 0))
    forth = back = panel
    for k in range(1, depth // 2 + 1):
        forth = lax.ppermute(forth, "z", [(i, (i + 1) % depth) for i in range(depth)])
        block = lax.dynamic_update_slice(block, forth, ((place + depth - k) % depth * each, 0))
        if k < depth - k:
            back = lax.ppermute(back, "z", [(i, (i - 1) % depth) for i in range(depth)])
            block = lax.dynamic_update_slice(block, back, ((place + k) % depth * each, 0))

    partner = lax.ppermute(panel, "c", swap)
    half = gram(which, panel, partner)
    pieces = lax.all_to_all(half.reshape(ring, -1, NB), plane, 0, 0, tiled=True)
    own = jnp.sum(pieces, axis=0)
    own = jnp.sum(spread(own, "z", depth).reshape((depth,) + own.shape), axis=0)
    mine = spread(own, plane, ring).reshape(half.shape)
    other = lax.ppermute(mine, "c", swap)
    top, top_inverse, tail, scales = factor_top(which, mine, other, total_rows)
    upper, ginv = factor_low(top, top_inverse, tail, scales)

    give = dot(lax.dynamic_slice(block, (0, (1 - core) * h), (depth * each, h)), trailing, ((0,), (0,)), high)
    got = lax.ppermute(give, "c", swap)
    keep = dot(lax.dynamic_slice(block, (0, core * h), (depth * each, h)), trailing, ((0,), (0,)), high)
    keep = lax.optimization_barrier(keep)
    pieces = lax.all_to_all((keep + got).reshape(ring, h // ring, -1), plane, 0, 0, tiled=True)
    own = jnp.sum(pieces, axis=0)
    near = spread(own, plane, ring).reshape(h, -1)
    far = lax.ppermute(near, "c", swap)

    weights = dot(lax.dynamic_slice(ginv, (core * h, 0), (h, B)), near, ((0,), (0,)))
    weights = weights + dot(lax.dynamic_slice(ginv, ((1 - core) * h, 0), (h, B)), far, ((0,), (0,)))
    residual = trailing - dot(block, weights, ((1,), (0,)), high)
    return (upper, residual)


def solution(mesh):
    row, col = mesh.devices.shape
    y = 8 if row == 64 else 2
    fine = Mesh(mesh.devices.reshape(row // (2 * y), y, 2, col), ("x", "y", "c", "z"))
    row_axes = ("x", "y", "c")
    return jax.shard_map(
        per_device,
        mesh=fine,
        in_specs=(P(row_axes + ("z",), None), P(row_axes, "z")),
        out_specs=(P(), P(row_axes, "z")),
        check_vma=False,
    )
```

```python
import functools
import math

import jax
import jax.numpy as jnp
from jax import lax
from jax.experimental import pallas as pl
from jax.experimental.pallas import tpu as pltpu
from jax.sharding import Mesh, PartitionSpec as P


HI = lax.Precision.HIGHEST
B = 512
NB = 128
F32 = jnp.float32


def gram_kernel(which, a_ref, b_ref, out_ref):
    h = B // 2

    def prod(rows, cols):
        total = None
        for ref in (a_ref, b_ref):
            term = lax.dot_general(
                ref[:, rows], ref[:, cols], (((0,), (0,)), ((), ())), precision=HI, preferred_element_type=F32
            )
            total = term if total is None else total + term
        return total

    def put(j, v):
        for i in range(v.shape[1] // NB):
            tiles = v[:, i * NB:(i + 1) * NB].reshape(h // 8, 8, NB)
            out_ref[:, 8 * (j + i):8 * (j + i + 1), :] = tiles

    @pl.when(which[0] == 0)
    def _():
        put(0, prod(slice(0, h), slice(0, 384)))

    @pl.when(which[0] != 0)
    def _():
        put(0, prod(slice(0, h), slice(384, B)))
        put(1, prod(slice(h, B), slice(h, B)))


def sub_row(v, j):
    return jnp.broadcast_to(v[j:j + 1, :], v.shape)


def tree(p):
    return ((p[0] + p[1]) + (p[2] + p[3])) + ((p[4] + p[5]) + (p[6] + p[7]))


def solve_strip(a, y, cols, sub):
    rows_r = rows_y = jnp.zeros_like(a)
    for j in range(0, 8, 2):
        h0, h1 = sub == j, sub == j + 1
        c0, c1 = cols[j], cols[j + 1]
        d0, b, d1 = sub_row(c0, j), sub_row(c1, j), sub_row(c1, j + 1)
        det = d0 * d1 - b * b
        rdet = 1.0 / det
        r0 = lax.rsqrt(d0)
        r1 = lax.rsqrt(det) * (d0 * r0)
        g = b * (r0 * r0)
        e0 = jnp.where(h0, -d1, jnp.where(h1, b, c0 * d1 - c1 * b))
        e1 = jnp.where(h0, b, jnp.where(h1, -d0, c1 * d0 - c0 * b))
        pair = h0 | h1

        def apply(v):
            v0, v1 = sub_row(v, j), sub_row(v, j + 1)
            return jnp.where(pair, 0.0, v) - (e0 * v0 + e1 * v1) * rdet, v0, v1

        a, a0, a1 = apply(a)
        y, y0, y1 = apply(y)
        rows_r = jnp.where(h0, a0 * r0, jnp.where(h1, (a1 - g * a0) * r1, rows_r))
        rows_y = jnp.where(h0, y0 * r0, jnp.where(h1, (y1 - g * y0) * r1, rows_y))
        for m in range(j + 2, 8):
            cols[m] = apply(cols[m])[0]
    return a, y, rows_r, rows_y


def factor_block(aug, inv, at):
    sub = lax.broadcasted_iota(jnp.int32, (8, NB), 0)
    lane = lax.broadcasted_iota(jnp.int32, (8, NB), 1)
    strips = range(NB // 8)
    a = [aug[at + 8 * t:at + 8 * t + 8, at:at + NB] for t in strips]
    y = [jnp.where(lane == sub + 8 * t, 1.0, 0.0).astype(F32) for t in strips]
    for s in strips:
        lanes = [slice(8 * s + j, 8 * s + j + 1) for j in range(8)]
        cols = [jnp.broadcast_to(a[s][:, c], (8, NB)) for c in lanes]
        av, yv, rows_r, rows_y = solve_strip(a[s], y[s], cols, sub)
        inv[8 * s:8 * s + 8, :] = rows_y
        inv[NB + 8 * s:NB + 8 * s + 8, :] = rows_r
        va = [sub_row(av, j) for j in range(8)]
        vy = [sub_row(yv, j) for j in range(8)]
        for t in range(s + 1, NB // 8):
            left = [jnp.broadcast_to(a[t][:, c], (8, NB)) for c in lanes]
            a[t] = a[t] - tree([u * v for u, v in zip(left, va)])
            y[t] = y[t] - tree([u * v for u, v in zip(left, vy)])


def run_block(aug, inv, at, width, done):
    factor_block(aug, inv, at)
    rows = slice(at, at + NB)
    end = width + done
    aug[rows, at + NB:end] = jnp.dot(
        inv[0:NB, :], aug[rows, at + NB:end], precision=HI, preferred_element_type=F32
    )
    aug[rows, end:end + NB] = inv[0:NB, :]
    for low in range(at + NB, width, NB):
        aug[low:low + NB, low:end + NB] -= lax.dot_general(
            aug[rows, low:low + NB], aug[rows, low:end + NB],
            (((0,), (0,)), ((), ())), precision=HI, preferred_element_type=F32,
        )


def triangle(inv):
    r = lax.broadcasted_iota(jnp.int32, (NB, NB), 0)
    c = lax.broadcasted_iota(jnp.int32, (NB, NB), 1)
    return jnp.where(c >= r, inv[NB:2 * NB, :], 0.0)


def top_kernel(scale, which, mine_ref, other_ref, r_out, m_out, tail_out, s_out, aug, inv):
    h = B // 2

    def load(lo, hi):
        def tiles(ref, i):
            return ref[:, 8 * i:8 * i + 8, :].reshape(h, NB)

        for i in range(3):
            aug[0:h, i * NB:(i + 1) * NB] = tiles(lo, i)
        aug[0:h, 384:B] = tiles(hi, 0)
        for i in range(2):
            aug[h:B, h + i * NB:h + (i + 1) * NB] = tiles(hi, 1 + i)

    @pl.when(which[0] == 0)
    def _():
        load(mine_ref, other_ref)

    @pl.when(which[0] != 0)
    def _():
        load(other_ref, mine_ref)

    eye = lax.broadcasted_iota(jnp.int32, (NB, NB), 0) == lax.broadcasted_iota(jnp.int32, (NB, NB), 1)
    col = []
    for at in range(0, B, NB):
        diag = jnp.where(eye, aug[at:at + NB, at:at + NB], 0.0)
        row = jnp.sum(diag, axis=0, keepdims=True)
        s_out[0:1, at:at + NB] = lax.rsqrt(row)
        s_out[1:2, at:at + NB] = row * lax.rsqrt(row) * scale
        col.append(lax.rsqrt(jnp.sum(diag, axis=1, keepdims=True)))
    for b in range(B // NB):
        rows, cols = slice(b * NB, (b + 1) * NB), slice(b * NB, B)
        aug[rows, cols] = aug[rows, cols] * col[b] * s_out[0:1, cols]
    aug[:, B:] = jnp.zeros((B, h), F32)

    for at in (0, NB):
        run_block(aug, inv, at, B, at)
        rows = slice(at, at + NB)
        r_out[rows, at:at + NB] = triangle(inv) * s_out[1:2, at:at + NB]
        r_out[rows, at + NB:B] = aug[rows, at + NB:B] * s_out[1:2, at + NB:B]
        m_out[rows, :] = aug[rows, B:] * s_out[0:1, 0:h]
    r_out[NB:h, 0:NB] = jnp.zeros((NB, NB), F32)
    tail_out[...] = aug[h:B, h:]


def low_kernel(which, top_ref, mtop_ref, tail_ref, s_ref, r_out, g_out, aug, inv, low):
    h = B // 2
    r_out[0:h, :] = top_ref[...]
    r_out[h:B, 0:h] = jnp.zeros((h, h), F32)
    aug[:, 0:B] = tail_ref[...]
    aug[:, B:] = jnp.zeros((h, h), F32)
    for at in (0, NB):
        run_block(aug, inv, at, h, h + at)
        rows = slice(at, at + NB)
        g = h + at
        r_out[g:g + NB, g:g + NB] = triangle(inv) * s_ref[1:2, g:g + NB]
        if g + NB < B:
            r_out[g:g + NB, g + NB:B] = aug[rows, at + NB:h] * s_ref[1:2, g + NB:B]
        low[rows, :] = aug[rows, h:] * s_ref[0:1, :]
    r_out[B - NB:B, h:B - NB] = jnp.zeros((NB, NB), F32)

    def square(a, b):
        return lax.dot_general(a, b, (((0,), (0,)), ((), ())), precision=HI, preferred_element_type=F32)

    upper = pl.ds(pl.multiple_of(which[0] * h, h), h)
    lower = pl.ds(pl.multiple_of((1 - which[0]) * h, h), h)
    g_out[upper, 0:h] = square(low[:, 0:h], low[:, 0:h]) + square(mtop_ref[...], mtop_ref[...])
    g_out[upper, h:B] = square(low[:, 0:h], low[:, h:B])
    g_out[lower, :] = square(low[:, h:B], low[...])


VM = pl.BlockSpec(memory_space=pltpu.VMEM)
SM = pl.BlockSpec(memory_space=pltpu.SMEM)


def gram(which, panel, partner):
    return pl.pallas_call(
        gram_kernel,
        out_shape=jax.ShapeDtypeStruct((B // 16, 24, NB), F32),
        in_specs=[SM, VM, VM],
        out_specs=VM,
        name="gram",
    )(which, panel, partner)


def factor_top(which, mine, other, total_rows):
    h = B // 2
    return pl.pallas_call(
        functools.partial(top_kernel, 1.0 / math.sqrt(total_rows)),
        out_shape=[jax.ShapeDtypeStruct(s, F32) for s in ((h, B), (h, h), (h, B), (8, B))],
        in_specs=[SM, VM, VM],
        out_specs=[VM] * 4,
        scratch_shapes=[pltpu.VMEM((B, B + h), F32), pltpu.VMEM((2 * NB, NB), F32)],
        name="factor_top",
    )(which, mine, other)


def factor_low(which, top, top_inverse, tail, scales):
    h = B // 2
    return pl.pallas_call(
        low_kernel,
        out_shape=[jax.ShapeDtypeStruct((B, B), F32)] * 2,
        in_specs=[SM] + [VM] * 4,
        out_specs=[VM] * 2,
        scratch_shapes=[pltpu.VMEM((h, h + B), F32), pltpu.VMEM((2 * NB, NB), F32), pltpu.VMEM((h, B), F32)],
        name="factor_low",
    )(which, top, top_inverse, tail, scales)


def dot(a, b, dims, precision=HI):
    return lax.dot_general(a, b, (dims, ((), ())), precision=precision, preferred_element_type=jnp.float32)


def spread(own, axes, parts):
    copies = jnp.broadcast_to(own[None], (parts,) + own.shape)
    return lax.all_to_all(copies, axes, 0, 0, tiled=True)


def per_device(panel, trailing):
    high = lax.Precision.HIGH
    plane = ("x", "y")
    ring, depth = lax.axis_size(plane), lax.axis_size("z")
    total_rows = panel.shape[0] * ring * depth * 2
    core = lax.axis_index("c")
    place = lax.axis_index("z")
    swap = [(0, 1), (1, 0)]
    h = B // 2
    each = panel.shape[0]
    which = jnp.full((1,), core, jnp.int32)

    block = jnp.zeros((depth * each, B), jnp.float32)
    block = lax.dynamic_update_slice(block, panel, (place * each, 0))
    forth = back = panel
    for k in range(1, depth // 2 + 1):
        forth = lax.ppermute(forth, "z", [(i, (i + 1) % depth) for i in range(depth)])
        block = lax.dynamic_update_slice(block, forth, ((place + depth - k) % depth * each, 0))
        if k < depth - k:
            back = lax.ppermute(back, "z", [(i, (i - 1) % depth) for i in range(depth)])
            block = lax.dynamic_update_slice(block, back, ((place + k) % depth * each, 0))

    partner = lax.ppermute(panel, "c", swap)
    half = gram(which, panel, partner)
    pieces = lax.all_to_all(half.reshape(ring, -1, NB), plane, 0, 0, tiled=True)
    own = jnp.sum(pieces, axis=0)
    own = jnp.sum(spread(own, "z", depth).reshape((depth,) + own.shape), axis=0)
    mine = spread(own, plane, ring).reshape(half.shape)
    other = lax.ppermute(mine, "c", swap)
    top, top_inverse, tail, scales = factor_top(which, mine, other, total_rows)
    upper, ginv = factor_low(which, top, top_inverse, tail, scales)

    give = dot(lax.dynamic_slice(block, (0, (1 - core) * h), (depth * each, h)), trailing, ((0,), (0,)), high)
    got = lax.ppermute(give, "c", swap)
    keep = dot(lax.dynamic_slice(block, (0, core * h), (depth * each, h)), trailing, ((0,), (0,)), high)
    keep = lax.optimization_barrier(keep)
    pieces = lax.all_to_all((keep + got).reshape(ring, h // ring, -1), plane, 0, 0, tiled=True)
    own = jnp.sum(pieces, axis=0)
    near = spread(own, plane, ring).reshape(h, -1)
    far = lax.ppermute(near, "c", swap)

    weights = dot(ginv[:h], near, ((0,), (0,)))
    weights = weights + dot(ginv[h:], far, ((0,), (0,)))
    residual = trailing - dot(block, weights, ((1,), (0,)), high)
    return (upper, residual)


def solution(mesh):
    row, col = mesh.devices.shape
    y = 8 if row == 64 else 2
    fine = Mesh(mesh.devices.reshape(row // (2 * y), y, 2, col), ("x", "y", "c", "z"))
    row_axes = ("x", "y", "c")
    return jax.shard_map(
        per_device,
        mesh=fine,
        in_specs=(P(row_axes + ("z",), None), P(row_axes, "z")),
        out_specs=(P(), P(row_axes, "z")),
        check_vma=False,
    )
```

```python
import functools
import math

import jax
import jax.numpy as jnp
from jax import lax
from jax.experimental import pallas as pl
from jax.experimental.pallas import tpu as pltpu
from jax.sharding import Mesh, PartitionSpec as P


HI = lax.Precision.HIGHEST
B = 512
NB = 128
F32 = jnp.float32


def gram_kernel(which, a_ref, b_ref, out_ref):
    h = B // 2

    def prod(rows, cols):
        total = None
        for ref in (a_ref, b_ref):
            term = lax.dot_general(
                ref[:, rows], ref[:, cols], (((0,), (0,)), ((), ())), precision=HI, preferred_element_type=F32
            )
            total = term if total is None else total + term
        return total

    def put(j, v):
        for i in range(v.shape[1] // NB):
            tiles = v[:, i * NB:(i + 1) * NB].reshape(h // 8, 8, NB)
            out_ref[:, 8 * (j + i):8 * (j + i + 1), :] = tiles

    @pl.when(which[0] == 0)
    def _():
        put(0, prod(slice(0, h), slice(0, 384)))

    @pl.when(which[0] != 0)
    def _():
        put(0, prod(slice(0, h), slice(384, B)))
        put(1, prod(slice(h, B), slice(h, B)))


def sub_row(v, j):
    return jnp.broadcast_to(v[j:j + 1, :], v.shape)


def tree(p):
    return ((p[0] + p[1]) + (p[2] + p[3])) + ((p[4] + p[5]) + (p[6] + p[7]))


def solve_strip(a, y, cols, sub):
    rows_r = rows_y = jnp.zeros_like(a)
    for j in range(0, 8, 2):
        h0, h1 = sub == j, sub == j + 1
        c0, c1 = cols[j], cols[j + 1]
        d0, b, d1 = sub_row(c0, j), sub_row(c1, j), sub_row(c1, j + 1)
        det = d0 * d1 - b * b
        rdet = 1.0 / det
        r0 = lax.rsqrt(d0)
        r1 = lax.rsqrt(det) * (d0 * r0)
        g = b * (r0 * r0)
        e0 = jnp.where(h0, -d1, jnp.where(h1, b, c0 * d1 - c1 * b))
        e1 = jnp.where(h0, b, jnp.where(h1, -d0, c1 * d0 - c0 * b))
        pair = h0 | h1

        def apply(v):
            v0, v1 = sub_row(v, j), sub_row(v, j + 1)
            return jnp.where(pair, 0.0, v) - (e0 * v0 + e1 * v1) * rdet, v0, v1

        a, a0, a1 = apply(a)
        y, y0, y1 = apply(y)
        rows_r = jnp.where(h0, a0 * r0, jnp.where(h1, (a1 - g * a0) * r1, rows_r))
        rows_y = jnp.where(h0, y0 * r0, jnp.where(h1, (y1 - g * y0) * r1, rows_y))
        for m in range(j + 2, 8):
            cols[m] = apply(cols[m])[0]
    return a, y, rows_r, rows_y


def factor_block(aug, inv, at):
    sub = lax.broadcasted_iota(jnp.int32, (8, NB), 0)
    lane = lax.broadcasted_iota(jnp.int32, (8, NB), 1)
    strips = range(NB // 8)
    a = [aug[at + 8 * t:at + 8 * t + 8, at:at + NB] for t in strips]
    y = [jnp.where(lane == sub + 8 * t, 1.0, 0.0).astype(F32) for t in strips]
    for s in strips:
        lanes = [slice(8 * s + j, 8 * s + j + 1) for j in range(8)]
        cols = [jnp.broadcast_to(a[s][:, c], (8, NB)) for c in lanes]
        av, yv, rows_r, rows_y = solve_strip(a[s], y[s], cols, sub)
        inv[8 * s:8 * s + 8, :] = rows_y
        inv[NB + 8 * s:NB + 8 * s + 8, :] = rows_r
        va = [sub_row(av, j) for j in range(8)]
        vy = [sub_row(yv, j) for j in range(8)]
        for t in range(s + 1, NB // 8):
            left = [jnp.broadcast_to(a[t][:, c], (8, NB)) for c in lanes]
            a[t] = a[t] - tree([u * v for u, v in zip(left, va)])
            y[t] = y[t] - tree([u * v for u, v in zip(left, vy)])


def run_block(aug, inv, at, width, done):
    factor_block(aug, inv, at)
    rows = slice(at, at + NB)
    end = width + done
    aug[rows, at + NB:end] = jnp.dot(
        inv[0:NB, :], aug[rows, at + NB:end], precision=HI, preferred_element_type=F32
    )
    aug[rows, end:end + NB] = inv[0:NB, :]
    for low in range(at + NB, width, NB):
        aug[low:low + NB, low:end + NB] -= lax.dot_general(
            aug[rows, low:low + NB], aug[rows, low:end + NB],
            (((0,), (0,)), ((), ())), precision=HI, preferred_element_type=F32,
        )


def triangle(inv):
    r = lax.broadcasted_iota(jnp.int32, (NB, NB), 0)
    c = lax.broadcasted_iota(jnp.int32, (NB, NB), 1)
    return jnp.where(c >= r, inv[NB:2 * NB, :], 0.0)


def top_kernel(scale, which, mine_ref, other_ref, r_out, m_out, tail_out, s_out, aug, inv):
    h = B // 2

    def load(lo, hi):
        def tiles(ref, i):
            return ref[:, 8 * i:8 * i + 8, :].reshape(h, NB)

        for i in range(3):
            aug[0:h, i * NB:(i + 1) * NB] = tiles(lo, i)
        aug[0:h, 384:B] = tiles(hi, 0)
        for i in range(2):
            aug[h:B, h + i * NB:h + (i + 1) * NB] = tiles(hi, 1 + i)

    @pl.when(which[0] == 0)
    def _():
        load(mine_ref, other_ref)

    @pl.when(which[0] != 0)
    def _():
        load(other_ref, mine_ref)

    eye = lax.broadcasted_iota(jnp.int32, (NB, NB), 0) == lax.broadcasted_iota(jnp.int32, (NB, NB), 1)
    col = []
    for at in range(0, B, NB):
        diag = jnp.where(eye, aug[at:at + NB, at:at + NB], 0.0)
        row = jnp.sum(diag, axis=0, keepdims=True)
        s_out[0:1, at:at + NB] = lax.rsqrt(row)
        s_out[1:2, at:at + NB] = row * lax.rsqrt(row) * scale
        col.append(lax.rsqrt(jnp.sum(diag, axis=1, keepdims=True)))
    for b in range(B // NB):
        rows, cols = slice(b * NB, (b + 1) * NB), slice(b * NB, B)
        aug[rows, cols] = aug[rows, cols] * col[b] * s_out[0:1, cols]
    aug[:, B:] = jnp.zeros((B, h), F32)

    for at in (0, NB):
        run_block(aug, inv, at, B, at)
        rows = slice(at, at + NB)
        r_out[rows, at:at + NB] = triangle(inv) * s_out[1:2, at:at + NB]
        r_out[rows, at + NB:B] = aug[rows, at + NB:B] * s_out[1:2, at + NB:B]
        m_out[rows, :] = aug[rows, B:] * s_out[0:1, 0:h]
    r_out[NB:h, 0:NB] = jnp.zeros((NB, NB), F32)
    tail_out[...] = aug[h:B, h:]


def low_kernel(which, top_ref, mtop_ref, tail_ref, s_ref, r_out, g_out, aug, inv, low):
    h = B // 2
    r_out[0:h, :] = top_ref[...]
    r_out[h:B, 0:h] = jnp.zeros((h, h), F32)
    aug[:, 0:B] = tail_ref[...]
    aug[:, B:] = jnp.zeros((h, h), F32)
    for at in (0, NB):
        run_block(aug, inv, at, h, h + at)
        rows = slice(at, at + NB)
        g = h + at
        r_out[g:g + NB, g:g + NB] = triangle(inv) * s_ref[1:2, g:g + NB]
        if g + NB < B:
            r_out[g:g + NB, g + NB:B] = aug[rows, at + NB:h] * s_ref[1:2, g + NB:B]
        low[rows, :] = aug[rows, h:] * s_ref[0:1, :]
    r_out[B - NB:B, h:B - NB] = jnp.zeros((NB, NB), F32)

    def square(a, b):
        return lax.dot_general(a, b, (((0,), (0,)), ((), ())), precision=HI, preferred_element_type=F32)

    upper = pl.ds(pl.multiple_of(which[0] * h, h), h)
    lower = pl.ds(pl.multiple_of((1 - which[0]) * h, h), h)
    g_out[upper, 0:h] = square(low[:, 0:h], low[:, 0:h]) + square(mtop_ref[...], mtop_ref[...])
    g_out[upper, h:B] = square(low[:, 0:h], low[:, h:B])
    g_out[lower, :] = square(low[:, h:B], low[...])


VM = pl.BlockSpec(memory_space=pltpu.VMEM)
SM = pl.BlockSpec(memory_space=pltpu.SMEM)


def gram(which, panel, partner):
    return pl.pallas_call(
        gram_kernel,
        out_shape=jax.ShapeDtypeStruct((B // 16, 24, NB), F32),
        in_specs=[SM, VM, VM],
        out_specs=VM,
        name="gram",
    )(which, panel, partner)


def factor_top(which, mine, other, total_rows):
    h = B // 2
    return pl.pallas_call(
        functools.partial(top_kernel, 1.0 / math.sqrt(total_rows)),
        out_shape=[jax.ShapeDtypeStruct(s, F32) for s in ((h, B), (h, h), (h, B), (8, B))],
        in_specs=[SM, VM, VM],
        out_specs=[VM] * 4,
        scratch_shapes=[pltpu.VMEM((B, B + h), F32), pltpu.VMEM((2 * NB, NB), F32)],
        name="factor_top",
    )(which, mine, other)


def factor_low(which, top, top_inverse, tail, scales):
    h = B // 2
    return pl.pallas_call(
        low_kernel,
        out_shape=[jax.ShapeDtypeStruct((B, B), F32)] * 2,
        in_specs=[SM] + [VM] * 4,
        out_specs=[VM] * 2,
        scratch_shapes=[pltpu.VMEM((h, h + B), F32), pltpu.VMEM((2 * NB, NB), F32), pltpu.VMEM((h, B), F32)],
        name="factor_low",
    )(which, top, top_inverse, tail, scales)


def dot(a, b, dims, precision=HI):
    return lax.dot_general(a, b, (dims, ((), ())), precision=precision, preferred_element_type=jnp.float32)


def spread(own, axes, parts):
    copies = jnp.broadcast_to(own[None], (parts,) + own.shape)
    return lax.all_to_all(copies, axes, 0, 0, tiled=True)


def gather_block(panel):
    depth, place, each = lax.axis_size("z"), lax.axis_index("z"), panel.shape[0]
    pairs = depth // 2
    odd, mine = place % 2, place // 2
    swaps = ([(i, i ^ 1) for i in range(depth)], [(i, (i + (1 if i % 2 else -1)) % depth) for i in range(depth)])
    other = lax.ppermute(panel, "z", swaps[0])
    held = jnp.where(odd == 0, jnp.concatenate([panel, other]), jnp.concatenate([other, panel]))
    block = jnp.zeros((depth * each, B), jnp.float32)
    block = lax.dynamic_update_slice(block, held, (mine * 2 * each, 0))
    step = 2 * odd - 1
    for k in range(2, pairs + 1):
        held = lax.ppermute(held, "z", swaps[(k + 1) % 2])
        back = (k // 2) * (step if k % 2 == 0 else -step)
        block = lax.dynamic_update_slice(block, held, ((mine + back + depth) % pairs * 2 * each, 0))
    return block


def per_device(panel, trailing):
    high = lax.Precision.HIGH
    plane = ("x", "y")
    ring, depth = lax.axis_size(plane), lax.axis_size("z")
    total_rows = panel.shape[0] * ring * depth * 2
    core = lax.axis_index("c")
    swap = [(0, 1), (1, 0)]
    h = B // 2
    each = panel.shape[0]
    which = jnp.full((1,), core, jnp.int32)

    block = gather_block(panel)

    partner = lax.ppermute(panel, "c", swap)
    half = gram(which, panel, partner)
    pieces = lax.all_to_all(half.reshape(ring, -1, NB), plane, 0, 0, tiled=True)
    own = jnp.sum(pieces, axis=0)
    own = jnp.sum(spread(own, "z", depth).reshape((depth,) + own.shape), axis=0)
    mine = spread(own, plane, ring).reshape(half.shape)
    other = lax.ppermute(mine, "c", swap)
    top, top_inverse, tail, scales = factor_top(which, mine, other, total_rows)
    upper, ginv = factor_low(which, top, top_inverse, tail, scales)

    give = dot(lax.dynamic_slice(block, (0, (1 - core) * h), (depth * each, h)), trailing, ((0,), (0,)), high)
    got = lax.ppermute(give, "c", swap)
    keep = dot(lax.dynamic_slice(block, (0, core * h), (depth * each, h)), trailing, ((0,), (0,)), high)
    keep = lax.optimization_barrier(keep)
    pieces = lax.all_to_all((keep + got).reshape(ring, h // ring, -1), plane, 0, 0, tiled=True)
    own = jnp.sum(pieces, axis=0)
    near = spread(own, plane, ring).reshape(h, -1)
    far = lax.ppermute(near, "c", swap)

    weights = dot(ginv[:h], near, ((0,), (0,)))
    weights = weights + dot(ginv[h:], far, ((0,), (0,)))
    residual = trailing - dot(block, weights, ((1,), (0,)), high)
    return (upper, residual)


def solution(mesh):
    row, col = mesh.devices.shape
    y = 8 if row == 64 else 2
    fine = Mesh(mesh.devices.reshape(row // (2 * y), y, 2, col), ("x", "y", "c", "z"))
    row_axes = ("x", "y", "c")
    return jax.shard_map(
        per_device,
        mesh=fine,
        in_specs=(P(row_axes + ("z",), None), P(row_axes, "z")),
        out_specs=(P(), P(row_axes, "z")),
        check_vma=False,
    )
```
